32 devices in a mesh: section: 4 (over z), dp: 2 (over x), tensor: 4 (over y, core).
Axes of the slice: x: 2, y: 2, z: 4, core: 2. Of those that a mesh axis runs over, the one named last changes fastest.
Arguments:
- sent: bfloat16 [8, 384, 6144], P('section', 'dp', 'tensor'), may hold values from -6 to 6
- stashed_inputs: bfloat16 [16, 96, 6144], P('section', 'dp', 'tensor'), may hold values from -6 to 6
- table: int32 [4, 4], P('section'), may hold values from 0 to 3, each once within a row
- embedded: bfloat16 [384, 6144], P('dp', 'tensor'), may hold values from -6 to 6
- loss_gradient: bfloat16 [384, 6144], P('dp', 'tensor'), may hold values from -6 to 6
- weight: bfloat16 [4, 6144, 6144], P('section', None, 'tensor'), may hold values from -0.078125 to 0.078125
- adapter_down_weight: bfloat16 [4, 6144, 128], P('section'), may hold values from -0.078125 to 0.078125
- adapter_up_weight: bfloat16 [4, 128, 6144], P('section', None, 'tensor'), may hold values from -0.5 to 0.5
Outputs:
- forward_output: bfloat16 [4, 384, 6144], P('section', 'dp', 'tensor')
- backward_output: bfloat16 [4, 384, 6144], P('section', 'dp', 'tensor')
- down_gradient: bfloat16 [4, 6144, 128], P('section', 'tensor')
- up_gradient: bfloat16 [4, 128, 6144], P('section', None, 'tensor')
The draws below stay inside these ranges and needn't reach their ends.
Inputs may be any that keep to these rules, and one draw needn't show every extreme that they name: Each row of table is a permutation of 0 to 3.
All inputs are finite; a program needn't handle non-finite values.
Results may differ from the reference program's by a relative error of at most 0.019.
Values may be sent and summed in bfloat16 or wider, within the bound.
A program may use at most 64 MiB of HBM per device.

```python
import jax
import jax.numpy as jnp
from jax import lax

MODEL_WIDTH = 6144
ADAPTER_RANK = 128
TOK_DEV = 192
TOKENS = 384
PIECE = 48
N_SECTION = 4
N_DP = 2
N_TENSOR = 4


def block_scale(own_key, dims, split, least, top_value):
    def one(dim, blocks):
        steps = jax.random.uniform(jax.random.fold_in(jax.random.fold_in(own_key, 6), dim), (blocks,), jnp.float32, least / len(split), top_value / len(split))
        return jnp.repeat(jnp.exp(steps), dims[dim] // blocks).reshape((-1,) + (1,) * (len(dims) - dim - 1))

    factor_of = one(*split[0])
    for cut in split[1:]:
        factor_of = factor_of * one(*cut)
    return factor_of


def normal_values(stream_key, extent, width, reach, pieces=(), kind=jnp.bfloat16):
    drawn = width * jax.random.normal(stream_key, extent, jnp.float32)
    if pieces:
        drawn = drawn * block_scale(stream_key, extent, pieces, -0.22, 0.18)
    return jnp.clip(drawn, -reach, reach).astype(kind)


def setup_inputs(seed: int = 0) -> dict:
    keys = jax.random.split(jax.random.key(seed), 9)
    return {
        "sent": normal_values(keys[0], (2 * N_SECTION, TOKENS, MODEL_WIDTH), 1.0, 6.0, ((0, 4), (1, 2), (2, 4))),
        "stashed_inputs": normal_values(keys[1], (N_SECTION * N_SECTION, PIECE * N_DP, MODEL_WIDTH), 1.0, 6.0, ((0, 4), (1, 2), (2, 4))),
        "table": jax.vmap(lambda own: jax.random.permutation(own, N_SECTION))(jax.random.split(keys[2], N_SECTION)).reshape((N_SECTION, N_SECTION)).astype(jnp.int32),
        "embedded": normal_values(keys[3], (TOKENS, MODEL_WIDTH), 1.0, 6.0, ((0, 2), (1, 4))),
        "loss_gradient": normal_values(keys[4], (TOKENS, MODEL_WIDTH), 1.0, 6.0, ((0, 2), (1, 4))),
        "weight": normal_values(keys[5], (N_SECTION, MODEL_WIDTH, MODEL_WIDTH), MODEL_WIDTH ** -0.5, 0.078125, ((0, 4), (2, 4))),
        "adapter_down_weight": normal_values(keys[6], (N_SECTION, MODEL_WIDTH, ADAPTER_RANK), MODEL_WIDTH ** -0.5, 0.078125, ((0, 4),)),
        "adapter_up_weight": normal_values(keys[7], (N_SECTION, ADAPTER_RANK, MODEL_WIDTH), ADAPTER_RANK ** -0.5, 0.5, ((0, 4), (2, 4))),
    }


coef = 0.7978845608028654


def gelu_pair(u):
    inner = coef * (u + 0.044715 * u * u * u)
    tanh_v = jnp.tanh(inner)
    value = 0.5 * u * (1.0 + tanh_v)
    slope = 0.5 * (1.0 + tanh_v) + 0.5 * u * (1.0 - tanh_v * tanh_v) * coef * (1.0 + 3.0 * 0.044715 * u * u)
    return value, slope


def round_back(value):
    rounded = lax.optimization_barrier(value.astype(jnp.bfloat16))
    return rounded.astype(jnp.float32)


def single_section(items):
    x_a, g_b, x_b, w_section, down_matrix, up = items
    h_a = jnp.dot(x_a, down_matrix, preferred_element_type=jnp.float32).astype(jnp.bfloat16)
    u_a = jnp.dot(x_a, w_section, preferred_element_type=jnp.float32) + jnp.dot(h_a, up, preferred_element_type=jnp.float32)
    value_a, unused = gelu_pair(u_a)
    y_a = (x_a.astype(jnp.float32) + value_a).astype(jnp.bfloat16)
    h_b = jnp.dot(x_b, down_matrix, preferred_element_type=jnp.float32).astype(jnp.bfloat16)
    u_b = jnp.dot(x_b, w_section, preferred_element_type=jnp.float32) + jnp.dot(h_b, up, preferred_element_type=jnp.float32)
    unused_b, slope_b = gelu_pair(u_b)
    scaled = (g_b.astype(jnp.float32) * slope_b).astype(jnp.bfloat16)
    scaled_parts = scaled.reshape(TOKENS, N_TENSOR, MODEL_WIDTH // N_TENSOR).astype(jnp.float32)
    w_parts = w_section.reshape(MODEL_WIDTH, N_TENSOR, MODEL_WIDTH // N_TENSOR).astype(jnp.float32)
    up_parts = up.reshape(ADAPTER_RANK, N_TENSOR, MODEL_WIDTH // N_TENSOR).astype(jnp.float32)
    low_parts = round_back(jnp.einsum('rtc,ktc->trk', scaled_parts, up_parts))
    low_terms = jnp.einsum('trk,dk->trd', low_parts, down_matrix.astype(jnp.float32))
    partial_value = jnp.einsum('rtc,dtc->trd', scaled_parts, w_parts) + low_terms
    input_grad = jnp.sum(round_back(partial_value), axis=0)
    low_grad = jnp.dot(scaled, up.T, preferred_element_type=jnp.float32).astype(jnp.bfloat16)
    dx_b = (g_b.astype(jnp.float32) + input_grad).astype(jnp.bfloat16)
    xb_rep = x_b.reshape(N_DP, TOK_DEV, MODEL_WIDTH).astype(jnp.float32)
    lg_rep = low_grad.reshape(N_DP, TOK_DEV, ADAPTER_RANK).astype(jnp.float32)
    hb_rep = h_b.reshape(N_DP, TOK_DEV, ADAPTER_RANK).astype(jnp.float32)
    sb_rep = scaled.reshape(N_DP, TOK_DEV, MODEL_WIDTH).astype(jnp.float32)
    down_part = jnp.einsum('rtd,rtk->rdk', xb_rep, lg_rep)
    up_part = jnp.einsum('rtk,rtd->rkd', hb_rep, sb_rep)
    down_gradient = jnp.sum(round_back(down_part), axis=0).astype(jnp.bfloat16)
    up_gradient = jnp.sum(round_back(up_part), axis=0).astype(jnp.bfloat16)
    return y_a, dx_b, down_gradient, up_gradient


def reference(sent, stashed_inputs, table, embedded, loss_gradient, weight, adapter_down_weight, adapter_up_weight):
    pairs = sent.reshape(N_SECTION, 2, TOKENS, MODEL_WIDTH)
    forward_input = jnp.concatenate([embedded[None], pairs[:-1, 1]], axis=0)
    incoming_gradient = jnp.concatenate([pairs[1:, 0], loss_gradient[None]], axis=0)
    inverse = jnp.argsort(table, axis=1).astype(jnp.int32)
    blocks = stashed_inputs.reshape(N_SECTION, N_SECTION, N_DP, PIECE, MODEL_WIDTH)
    holders = jnp.broadcast_to(jnp.arange(N_SECTION, dtype=jnp.int32)[None, :], (N_SECTION, N_SECTION))
    picked = blocks[holders, inverse.T]
    backward_input = jnp.transpose(picked, (0, 2, 1, 3, 4)).reshape(N_SECTION, TOKENS, MODEL_WIDTH)
    forward_output, backward_output, down_gradient, up_gradient = lax.map(single_section, (forward_input, incoming_gradient, backward_input, weight, adapter_down_weight, adapter_up_weight))
    return forward_output, backward_output, down_gradient, up_gradient
```

```python
import functools

import jax
import jax.numpy as jnp
from jax import lax
from jax.experimental import pallas as pl
from jax.experimental.pallas import tpu as pltpu
from jax.sharding import PartitionSpec as P

coef = 0.7978845608028654


def shifted(block, axis, distance):
    devices = range(lax.axis_size(axis))
    route = [(i - distance, i) for i in devices if i - distance in devices]
    return lax.ppermute(block, axis, route)


def gelu_pair(u):
    inner = coef * (u + 0.044715 * u * u * u)
    tanh_v = jnp.tanh(inner)
    value = 0.5 * u * (1.0 + tanh_v)
    slope = 0.5 * (1.0 + tanh_v) + 0.5 * u * (1.0 - tanh_v * tanh_v) * coef * (
        1.0 + 3.0 * 0.044715 * u * u
    )
    return (value, slope)


def on_device(
    sent,
    stashed_inputs,
    table,
    embedded,
    loss_gradient,
    weight,
    adapter_down_weight,
    adapter_up_weight,
):
    section = lax.axis_index("section")
    sections = lax.axis_size("section")
    w_section = weight[0]
    down_matrix = adapter_down_weight[0]
    up_matrix = adapter_up_weight[0]
    below = shifted(sent[1], "section", 1)
    above = shifted(sent[0], "section", -1)
    forward_input = jnp.where(section == 0, embedded, below)
    incoming_gradient = jnp.where(section == sections - 1, loss_gradient, above)
    order = jnp.argsort(table[0])
    arranged = jnp.take(stashed_inputs, order, axis=0)
    fetched = lax.all_to_all(arranged, "section", split_axis=0, concat_axis=0, tiled=True)
    backward_input = fetched.reshape(-1, fetched.shape[-1])
    full_a, full_b = (
        lax.all_gather(forward_input, "tensor", axis=1, tiled=True),
        lax.all_gather(backward_input, "tensor", axis=1, tiled=True),
    )
    main_a = jnp.dot(full_a, w_section, preferred_element_type=jnp.float32)
    h_a = jnp.dot(full_a, down_matrix, preferred_element_type=jnp.float32).astype(jnp.bfloat16)
    u_a = main_a + jnp.dot(h_a, up_matrix, preferred_element_type=jnp.float32)
    value_a, unused = gelu_pair(u_a)
    forward_output = (forward_input.astype(jnp.float32) + value_a).astype(jnp.bfloat16)
    h_b = jnp.dot(full_b, down_matrix, preferred_element_type=jnp.float32).astype(jnp.bfloat16)
    u_b = jnp.dot(full_b, w_section, preferred_element_type=jnp.float32) + jnp.dot(
        h_b, up_matrix, preferred_element_type=jnp.float32
    )
    unused_b, slope_b = gelu_pair(u_b)
    scaled = (incoming_gradient.astype(jnp.float32) * slope_b).astype(jnp.bfloat16)
    low_part = lax.dot_general(
        scaled, up_matrix, (((1,), (1,)), ((), ())), preferred_element_type=jnp.float32
    )
    low_piece = low_part.astype(jnp.bfloat16)
    partial_value = lax.dot_general(
        scaled, w_section, (((1,), (1,)), ((), ())), preferred_element_type=jnp.float32
    )
    partial_value = partial_value + lax.dot_general(
        low_piece, down_matrix, (((1,), (1,)), ((), ())), preferred_element_type=jnp.float32
    )
    input_grad = lax.psum_scatter(
        partial_value.astype(jnp.bfloat16), "tensor", scatter_dimension=1, tiled=True
    ).astype(jnp.float32)
    backward_output = (incoming_gradient.astype(jnp.float32) + input_grad).astype(jnp.bfloat16)
    low_grad = lax.psum(low_part.astype(jnp.bfloat16), "tensor")
    down_term = lax.dot_general(
        backward_input, low_grad, (((0,), (0,)), ((), ())), preferred_element_type=jnp.float32
    )
    up_term = lax.dot_general(
        h_b, scaled, (((0,), (0,)), ((), ())), preferred_element_type=jnp.float32
    )
    down_sum, up_sum = (
        lax.psum(down_term.astype(jnp.bfloat16), "dp").astype(jnp.float32),
        lax.psum(up_term.astype(jnp.bfloat16), "dp").astype(jnp.float32),
    )
    down_gradient = down_sum.astype(jnp.bfloat16)
    up_gradient = up_sum.astype(jnp.bfloat16)
    return (forward_output[None], backward_output[None], down_gradient[None], up_gradient[None])


F32 = jnp.float32
BF16 = jnp.bfloat16
MESH = pl.DeviceIdType.MESH


def dot_nn(a, b):
    return lax.dot_general(a, b, (((1,), (0,)), ((), ())), preferred_element_type=F32)


def dot_nt(a, b):
    return lax.dot_general(a, b, (((1,), (1,)), ((), ())), preferred_element_type=F32)


def dot_tn(a, b):
    return lax.dot_general(a, b, (((0,), (0,)), ((), ())), preferred_element_type=F32)


def window_kernel(
    sections, tile,
    sent, stash, table, embedded, loss, weight, down, up,
    out_f, out_b, out_d, out_u,
    w, dn, upv, xa, xb, g, arranged, u, ua, scaled, low, lowr, hb,
    p_send, q_send, o_send, p_recv, q_recv, o_recv, own,
    du_send, du_recv, dd_send, dd_recv,
    w_sem, d_sem, loc_sem, ex_s, ex_r, az_s, az_r, gz_s, gz_r,
    bx_s, bx_r, ax_s, ax_r, low_s, low_r, p_s, p_r, q_s, q_r, o_s, o_r, dp_s, dp_r,
):
    S = sections
    s = lax.axis_index("section")
    d = lax.axis_index("dp")
    t = lax.axis_index("tensor")
    t1 = t + 1 - 2 * (t % 2)
    t2 = (t + 2) % 4
    t3 = (t1 + 2) % 4
    rel = [t, t1, t2, t3]
    piece, cols = stash.shape[1], stash.shape[2]
    rows = S * piece
    tiles = cols // tile

    def remote(src, dst, ss, rs, **device):
        return pltpu.make_async_remote_copy(
            src_ref=src, dst_ref=dst, send_sem=ss, recv_sem=rs,
            device_id=device, device_id_type=MESH)

    emb_copy = pltpu.make_async_copy(embedded, xa.at[0], loc_sem.at[0])
    loss_copy = pltpu.make_async_copy(loss, g, loc_sem.at[1])
    up_copy = pltpu.make_async_copy(up, upv, loc_sem.at[2])
    w_copies = [pltpu.make_async_copy(weight.at[rel[r]], w.at[r], w_sem.at[r]) for r in range(4)]
    d_copies = [pltpu.make_async_copy(down.at[rel[r]], dn.at[r], d_sem.at[r]) for r in range(4)]

    barrier = pltpu.get_barrier_semaphore()
    for j in range(1, S):
        pl.semaphore_signal(barrier, inc=1, device_id={"section": (s + j) % S}, device_id_type=MESH)
    for r in range(1, 4):
        pl.semaphore_signal(barrier, inc=1, device_id={"tensor": rel[r]}, device_id_type=MESH)
    pl.semaphore_signal(barrier, inc=1, device_id={"dp": 1 - d}, device_id_type=MESH)

    for j in range(S):
        dest = (s + j) % S
        k = jnp.int32(0)
        for i in range(S):
            k = jnp.where(table[0, i] == dest, i, k)
        if j == 0:
            xb[0, s] = stash[k]
        else:
            arranged[j] = stash[k]
    pl.semaphore_wait(barrier, S + 3)

    ex = [None] + [
        remote(arranged.at[j], xb.at[0, s], ex_s.at[j], ex_r.at[j], section=(s + j) % S)
        for j in range(1, S)
    ]
    for j in EX_ORDER(S):
        ex[j].start()

    @pl.when(s == 0)
    def _():
        emb_copy.start()

    @pl.when(s == S - 1)
    def _():
        loss_copy.start()

    for r in range(4):
        d_copies[r].start()
        w_copies[r].start()
    up_copy.start()

    az = [remote(sent.at[1, c], xa.at[0, c], az_s.at[c], az_r.at[c], section=(s + 1) % S) for c in range(S)]
    gz = remote(sent.at[0], g, gz_s.at[0], gz_r.at[0], section=(s + S - 1) % S)

    @pl.when(s < S - 1)
    def _():
        for c in range(S):
            az[c].start()

    @pl.when(s > 0)
    def _():
        gz.start()

    def hops(x, c, sem_s, sem_r, i):
        return (
            remote(x.at[0, c], x.at[1, c], sem_s.at[0, i], sem_r.at[0, i], tensor=t1),
            remote(x.at[0, c], x.at[2, c], sem_s.at[1, i], sem_r.at[1, i], tensor=t2),
            remote(x.at[2, c], x.at[3, c], sem_s.at[2, i], sem_r.at[2, i], tensor=t1),
        )

    b_list = [0] + WAIT_ORDER(S)
    bh = [hops(xb, (s + S - j) % S, bx_s, bx_r, i) for i, j in enumerate(b_list)]
    ah = [hops(xa, c, ax_s, ax_r, c) for c in range(S)]

    def b_piece(i):
        j = b_list[i]
        if j:
            src = (s + S - j) % S
            remote(arranged.at[j], xb.at[0, src], ex_s.at[j], ex_r.at[j], section=src).wait_recv()
        bh[i][1].start()
        bh[i][0].start()

    def b_pass(i):
        bh[i][1].wait_recv()
        bh[i][2].start()

    def a_piece(c):
        if c == 0:
            @pl.when(s == 0)
            def _():
                emb_copy.wait()

        @pl.when(s > 0)
        def _():
            az[c].wait_recv()
        ah[c][1].start()
        ah[c][0].start()

    def a_pass(c):
        ah[c][1].wait_recv()
        ah[c][2].start()

    def forward(x, r, acc, first):
        lhs = x.at[r]

        def body(n, carry):
            at = pl.ds(pl.multiple_of(n * tile, tile), tile)
            val = dot_nn(lhs[...].reshape(rows, cols), w[r, :, at])
            if first:
                acc[n] = val
            else:
                acc[n] = acc[n] + val
            return carry
        lax.fori_loop(0, tiles, body, 0)

    def low_of(x, r):
        return dot_nn(x[r].reshape(rows, cols), dn[r])

    for i in range(S):
        b_piece(i)
        if i >= 1:
            b_pass(i - 1)

    d_copies[0].wait()
    w_copies[0].wait()
    forward(xb, 0, u, True)
    h = low_of(xb, 0)
    b_pass(S - 1)
    a_piece(0)
    for i in range(S):
        bh[i][0].wait_recv()
    d_copies[1].wait()
    w_copies[1].wait()
    forward(xb, 1, u, False)
    h = h + low_of(xb, 1)
    a_piece(1)
    d_copies[2].wait()
    w_copies[2].wait()
    forward(xb, 2, u, False)
    h = h + low_of(xb, 2)
    for i in range(S):
        bh[i][2].wait_recv()
    d_copies[3].wait()
    w_copies[3].wait()
    forward(xb, 3, u, False)
    h = h + low_of(xb, 3)
    hb[...] = h.astype(BF16)
    a_pass(0)
    for c in range(2, S):
        a_piece(c)
        a_pass(c - 1)
    up_copy.wait()

    def slope_body(n, carry):
        at = pl.ds(pl.multiple_of(n * tile, tile), tile)
        unused, slope = gelu_pair(u[n] + dot_nn(hb[...], upv[:, at]))
        u[n] = slope
        return carry
    lax.fori_loop(0, tiles, slope_body, 0)

    @pl.when(s == S - 1)
    def _():
        loss_copy.wait()

    @pl.when(s < S - 1)
    def _():
        gz.wait_recv()

    def scale_body(n, carry):
        at = pl.ds(pl.multiple_of(n * tile, tile), tile)
        scaled[:, at] = (g[:, :, at].reshape(rows, tile).astype(F32) * u[n]).astype(BF16)
        return carry
    lax.fori_loop(0, tiles, scale_body, 0)

    low[...] = dot_nt(scaled[...], upv[...]).astype(BF16)
    lows = [None] + [
        remote(low, lowr.at[r], low_s.at[r], low_r.at[r], tensor=rel[r]) for r in range(1, 4)
    ]
    for r in (2, 3, 1):
        lows[r].start()

    def up_body(n, carry):
        at = pl.ds(pl.multiple_of(n * tile, tile), tile)
        du_send[:, at] = dot_tn(hb[...], scaled[:, at]).astype(BF16)
        return carry
    lax.fori_loop(0, tiles, up_body, 0)
    du = remote(du_send, du_recv, dp_s.at[0], dp_r.at[0], dp=1 - d)
    du.start()

    def partial(r, n):
        at = pl.ds(pl.multiple_of(n * tile, tile), tile)
        return dot_nt(scaled[...], w[r, at, :]) + dot_nt(low[...], dn[r, at, :])

    def p_copy(n):
        return remote(p_send.at[n], p_recv.at[n], p_s.at[n], p_r.at[n], tensor=t1)

    def q_copy(n):
        return remote(q_send.at[n], q_recv.at[n], q_s.at[n], q_r.at[n], tensor=t2)

    def o_copy(n):
        return remote(o_send.at[n], o_recv.at[n], o_s.at[n], o_r.at[n], tensor=t1)

    def p_body(n, carry):
        p_send[n] = partial(3, n).astype(BF16)
        p_copy(n).start()
        return carry
    lax.fori_loop(0, tiles, p_body, 0)

    def q_body(n, carry):
        mine = partial(2, n)
        p_copy(n).wait_recv()
        q_send[n] = (mine + p_recv[n].astype(F32)).astype(BF16)
        q_copy(n).start()
        return carry
    lax.fori_loop(0, tiles, q_body, 0)
    a_pass(S - 1)

    total = low[...].astype(F32)
    for r in range(1, 4):
        lows[r].wait_recv()
        total = total + lowr[r].astype(F32)
    lowr[0] = total.astype(BF16)
    dd_send[...] = dot_tn(xb[0].reshape(rows, cols), lowr[0]).astype(BF16)
    dd = remote(dd_send, dd_recv, dp_s.at[1], dp_r.at[1], dp=1 - d)
    dd.start()

    def o_body(n, carry):
        o_send[n] = partial(1, n).astype(BF16)
        o_copy(n).start()
        return carry
    lax.fori_loop(0, tiles, o_body, 0)

    def own_body(n, carry):
        own[n] = partial(0, n)
        return carry
    lax.fori_loop(0, tiles, own_body, 0)

    forward(xa, 0, ua, True)
    h = low_of(xa, 0)
    for c in range(S):
        ah[c][0].wait_recv()
    forward(xa, 1, ua, False)
    h = h + low_of(xa, 1)
    forward(xa, 2, ua, False)
    h = h + low_of(xa, 2)
    for c in range(S):
        ah[c][2].wait_recv()
    forward(xa, 3, ua, False)
    h = h + low_of(xa, 3)
    ha = h.astype(BF16)
    hb2 = lowr.at[1]
    hb2[...] = ha

    def out_body(n, carry):
        at = pl.ds(pl.multiple_of(n * tile, tile), tile)
        value, unused = gelu_pair(ua[n] + dot_nn(lowr[1], upv[:, at]))
        base = xa[0, :, :, at].reshape(rows, tile).astype(F32)
        out_f[:, at] = (base + value).astype(BF16)
        return carry
    lax.fori_loop(0, tiles, out_body, 0)

    du.wait_recv()
    out_u[...] = (du_send[...].astype(F32) + du_recv[...].astype(F32)).astype(BF16)

    for n in range(tiles):
        o_copy(n).wait_recv()
        q_copy(n).wait_recv()
        at = pl.ds(n * tile, tile)
        total = own[n] + o_recv[n].astype(F32) + q_recv[n].astype(F32)
        out_b[:, at] = (g[:, :, at].reshape(rows, tile).astype(F32) + total).astype(BF16)

    dd.wait_recv()
    out_d[...] = (dd_send[...].astype(F32) + dd_recv[...].astype(F32)).astype(BF16)

    for j in range(1, S):
        ex[j].wait_send()

    @pl.when(s < S - 1)
    def _():
        for c in range(S):
            az[c].wait_send()

    @pl.when(s > 0)
    def _():
        gz.wait_send()
    for i in range(S):
        for hop in range(3):
            bh[i][hop].wait_send()
            ah[i][hop].wait_send()
    for r in range(1, 4):
        lows[r].wait_send()
    for n in range(tiles):
        p_copy(n).wait_send()
        q_copy(n).wait_send()
        o_copy(n).wait_send()
    du.wait_send()
    dd.wait_send()


def EX_ORDER(S):
    return sorted(range(1, S), key=lambda j: (-min(j, S - j), j))


def WAIT_ORDER(S):
    return sorted(range(1, S), key=lambda j: (min(j, S - j), j))


def fused_on_device(sent, stash, table, embedded, loss, weight, down, up):
    S = lax.axis_size("section")
    piece, cols = stash.shape[1], stash.shape[2]
    rows, rank = S * piece, up.shape[1]
    tile = next(k for k in (512, 256, 128) if cols % k == 0)
    tiles = cols // tile
    any_space = pl.BlockSpec(memory_space=pl.ANY)
    vmem = pl.BlockSpec(memory_space=pltpu.VMEM)
    smem = pl.BlockSpec(memory_space=pltpu.SMEM)
    V = pltpu.VMEM
    dma = lambda *shape: pltpu.SemaphoreType.DMA(shape)
    block = (tiles, rows, tile)
    outs = pl.pallas_call(
        functools.partial(window_kernel, S, tile),
        out_shape=(
            jax.ShapeDtypeStruct((rows, cols), BF16),
            jax.ShapeDtypeStruct((rows, cols), BF16),
            jax.ShapeDtypeStruct((cols, rank), BF16),
            jax.ShapeDtypeStruct((rank, cols), BF16),
        ),
        in_specs=[any_space, vmem, smem, any_space, any_space, any_space, any_space, any_space],
        out_specs=(vmem,) * 4,
        scratch_shapes=[
            V((4, cols, cols), BF16), V((4, cols, rank), BF16), V((rank, cols), BF16),
            V((4, S, piece, cols), BF16), V((4, S, piece, cols), BF16),
            V((S, piece, cols), BF16), V((S, piece, cols), BF16),
            V(block, F32), V(block, F32), V((rows, cols), BF16),
            V((rows, rank), BF16), V((4, rows, rank), BF16), V((rows, rank), BF16),
            V(block, BF16), V(block, BF16), V(block, BF16),
            V(block, BF16), V(block, BF16), V(block, BF16), V(block, F32),
            V((rank, cols), BF16), V((rank, cols), BF16),
            V((cols, rank), BF16), V((cols, rank), BF16),
            dma(4), dma(4), dma(3), dma(S), dma(S), dma(S), dma(S), dma(1), dma(1),
            dma(3, S), dma(3, S), dma(3, S), dma(3, S), dma(4), dma(4),
            dma(tiles), dma(tiles), dma(tiles), dma(tiles), dma(tiles), dma(tiles),
            dma(2), dma(2),
        ],
        compiler_params=pltpu.CompilerParams(
            collective_id=0, has_side_effects=True, vmem_limit_bytes=62 * 1024 * 1024),
    )(
        sent.reshape(2, S, piece, cols), stash, table,
        embedded.reshape(S, piece, cols), loss.reshape(S, piece, cols),
        weight.reshape(4, cols, cols), down.reshape(4, cols, rank), up[0],
    )
    return tuple(o[None] for o in outs)


def solution(mesh):
    placed = (
        P("section", "dp", "tensor"),
        P("section", "dp", "tensor"),
        P("section", None),
        P("dp", "tensor"),
        P("dp", "tensor"),
        P("section", None, "tensor"),
        P("section", None, None),
        P("section", None, "tensor"),
    )
    def program(*args):
        rows = args[1].shape[1] // mesh.shape["dp"]
        cols = args[1].shape[2] // mesh.shape["tensor"]
        fits = (
            mesh.shape["tensor"] == 4 and mesh.shape["dp"] == 2
            and rows % 16 == 0 and cols % 128 == 0
        )
        return sharded(fused_on_device if fits else on_device)(*args)

    def sharded(body):
      return jax.shard_map(
        body,
        mesh=mesh,
        in_specs=placed,
        out_specs=(
            P("section", "dp", "tensor"),
            P("section", "dp", "tensor"),
            P("section", "tensor", None),
            P("section", None, "tensor"),
        ),
        check_vma=False,
    )

    return program
```

```python
import functools

import jax
import jax.numpy as jnp
from jax import lax
from jax.experimental import pallas as pl
from jax.experimental.pallas import tpu as pltpu
from jax.sharding import PartitionSpec as P

coef = 0.7978845608028654


def shifted(block, axis, distance):
    devices = range(lax.axis_size(axis))
    route = [(i - distance, i) for i in devices if i - distance in devices]
    return lax.ppermute(block, axis, route)


def gelu_pair(u):
    inner = coef * (u + 0.044715 * u * u * u)
    tanh_v = jnp.tanh(inner)
    value = 0.5 * u * (1.0 + tanh_v)
    slope = 0.5 * (1.0 + tanh_v) + 0.5 * u * (1.0 - tanh_v * tanh_v) * coef * (
        1.0 + 3.0 * 0.044715 * u * u
    )
    return (value, slope)


def on_device(
    sent,
    stashed_inputs,
    table,
    embedded,
    loss_gradient,
    weight,
    adapter_down_weight,
    adapter_up_weight,
):
    section = lax.axis_index("section")
    sections = lax.axis_size("section")
    w_section = weight[0]
    down_matrix = adapter_down_weight[0]
    up_matrix = adapter_up_weight[0]
    below = shifted(sent[1], "section", 1)
    above = shifted(sent[0], "section", -1)
    forward_input = jnp.where(section == 0, embedded, below)
    incoming_gradient = jnp.where(section == sections - 1, loss_gradient, above)
    order = jnp.argsort(table[0])
    arranged = jnp.take(stashed_inputs, order, axis=0)
    fetched = lax.all_to_all(arranged, "section", split_axis=0, concat_axis=0, tiled=True)
    backward_input = fetched.reshape(-1, fetched.shape[-1])
    full_a, full_b = (
        lax.all_gather(forward_input, "tensor", axis=1, tiled=True),
        lax.all_gather(backward_input, "tensor", axis=1, tiled=True),
    )
    main_a = jnp.dot(full_a, w_section, preferred_element_type=jnp.float32)
    h_a = jnp.dot(full_a, down_matrix, preferred_element_type=jnp.float32).astype(jnp.bfloat16)
    u_a = main_a + jnp.dot(h_a, up_matrix, preferred_element_type=jnp.float32)
    value_a, unused = gelu_pair(u_a)
    forward_output = (forward_input.astype(jnp.float32) + value_a).astype(jnp.bfloat16)
    h_b = jnp.dot(full_b, down_matrix, preferred_element_type=jnp.float32).astype(jnp.bfloat16)
    u_b = jnp.dot(full_b, w_section, preferred_element_type=jnp.float32) + jnp.dot(
        h_b, up_matrix, preferred_element_type=jnp.float32
    )
    unused_b, slope_b = gelu_pair(u_b)
    scaled = (incoming_gradient.astype(jnp.float32) * slope_b).astype(jnp.bfloat16)
    low_part = lax.dot_general(
        scaled, up_matrix, (((1,), (1,)), ((), ())), preferred_element_type=jnp.float32
    )
    low_piece = low_part.astype(jnp.bfloat16)
    partial_value = lax.dot_general(
        scaled, w_section, (((1,), (1,)), ((), ())), preferred_element_type=jnp.float32
    )
    partial_value = partial_value + lax.dot_general(
        low_piece, down_matrix, (((1,), (1,)), ((), ())), preferred_element_type=jnp.float32
    )
    input_grad = lax.psum_scatter(
        partial_value.astype(jnp.bfloat16), "tensor", scatter_dimension=1, tiled=True
    ).astype(jnp.float32)
    backward_output = (incoming_gradient.astype(jnp.float32) + input_grad).astype(jnp.bfloat16)
    low_grad = lax.psum(low_part.astype(jnp.bfloat16), "tensor")
    down_term = lax.dot_general(
        backward_input, low_grad, (((0,), (0,)), ((), ())), preferred_element_type=jnp.float32
    )
    up_term = lax.dot_general(
        h_b, scaled, (((0,), (0,)), ((), ())), preferred_element_type=jnp.float32
    )
    down_sum, up_sum = (
        lax.psum(down_term.astype(jnp.bfloat16), "dp").astype(jnp.float32),
        lax.psum(up_term.astype(jnp.bfloat16), "dp").astype(jnp.float32),
    )
    down_gradient = down_sum.astype(jnp.bfloat16)
    up_gradient = up_sum.astype(jnp.bfloat16)
    return (forward_output[None], backward_output[None], down_gradient[None], up_gradient[None])


F32 = jnp.float32
BF16 = jnp.bfloat16
MESH = pl.DeviceIdType.MESH


def dot_nn(a, b):
    return lax.dot_general(a, b, (((1,), (0,)), ((), ())), preferred_element_type=F32)


def dot_nt(a, b):
    return lax.dot_general(a, b, (((1,), (1,)), ((), ())), preferred_element_type=F32)


def dot_tn(a, b):
    return lax.dot_general(a, b, (((0,), (0,)), ((), ())), preferred_element_type=F32)


def window_kernel(
    sections, tile,
    sent, stash_hbm, table, embedded, loss, weight, down, up,
    out_f, out_b, out_d, out_u,
    stash_v, w, dn, upv, xa, xb, g, arranged, u, ua, scaled, low, lowr, hb,
    p_send, q_send, o_send, p_recv, q_recv, o_recv, own,
    du_send, du_recv, xo, lg, lg_recv,
    w_sem, d_sem, loc_sem, ex_s, ex_r, az_s, az_r, gz_s, gz_r,
    xo_s, xo_r, bx_s, bx_r, ax_s, ax_r, low_s, low_r, p_s, p_r, q_s, q_r, o_s, o_r, dp_s, dp_r,
):
    S = sections
    s = lax.axis_index("section")
    d = lax.axis_index("dp")
    t = lax.axis_index("tensor")
    t1 = t + 1 - 2 * (t % 2)
    t2 = (t + 2) % 4
    t3 = (t1 + 2) % 4
    rel = [t, t1, t2, t3]
    piece, cols = stash_v.shape[1], stash_v.shape[2]
    rows = S * piece
    tiles = cols // tile
    stash_copy = pltpu.make_async_copy(stash_hbm, stash_v, loc_sem.at[0])
    stash_copy.start()

    def remote(src, dst, ss, rs, **device):
        return pltpu.make_async_remote_copy(
            src_ref=src, dst_ref=dst, send_sem=ss, recv_sem=rs,
            device_id=device, device_id_type=MESH)

    emb_copy = pltpu.make_async_copy(embedded, xa.at[0], loc_sem.at[3])
    loss_copy = pltpu.make_async_copy(loss, g, loc_sem.at[1])
    up_copy = pltpu.make_async_copy(up, upv, loc_sem.at[2])
    w_copies = [pltpu.make_async_copy(weight.at[rel[r]], w.at[r], w_sem.at[r]) for r in range(4)]
    d_copies = [pltpu.make_async_copy(down.at[rel[r]], dn.at[r], d_sem.at[r]) for r in range(4)]

    barrier = pltpu.get_barrier_semaphore()
    for j in range(1, S):
        pl.semaphore_signal(barrier, inc=1, device_id={"section": (s + j) % S}, device_id_type=MESH)
    for r in range(1, 4):
        pl.semaphore_signal(barrier, inc=1, device_id={"tensor": rel[r]}, device_id_type=MESH)
    pl.semaphore_signal(barrier, inc=1, device_id={"dp": 1 - d}, device_id_type=MESH)

    stash_copy.wait()
    for j in range(S):
        dest = (s + j) % S
        k = jnp.int32(0)
        for i in range(S):
            k = jnp.where(table[0, i] == dest, i, k)
        if j == 0:
            xb[0, s] = stash_v[k]
        else:
            arranged[j] = stash_v[k]
    pl.semaphore_wait(barrier, S + 3)

    ex = [None] + [
        remote(arranged.at[j], xb.at[0, s], ex_s.at[j], ex_r.at[j], section=(s + j) % S)
        for j in range(1, S)
    ]
    for j in EX_ORDER(S):
        ex[j].start()

    @pl.when(s == 0)
    def _():
        emb_copy.start()

    @pl.when(s == S - 1)
    def _():
        loss_copy.start()

    for r in range(4):
        d_copies[r].start()
        w_copies[r].start()
    up_copy.start()

    az = [remote(sent.at[1, c], xa.at[0, c], az_s.at[c], az_r.at[c], section=(s + 1) % S) for c in range(S)]
    gz = remote(sent.at[0], g, gz_s.at[0], gz_r.at[0], section=(s + S - 1) % S)

    @pl.when(s < S - 1)
    def _():
        for c in range(S):
            az[c].start()

    @pl.when(s > 0)
    def _():
        gz.start()

    def hops(x, c, sem_s, sem_r, i):
        return (
            remote(x.at[0, c], x.at[1, c], sem_s.at[0, i], sem_r.at[0, i], tensor=t1),
            remote(x.at[0, c], x.at[2, c], sem_s.at[1, i], sem_r.at[1, i], tensor=t2),
            remote(x.at[2, c], x.at[3, c], sem_s.at[2, i], sem_r.at[2, i], tensor=t1),
        )

    b_list = [0] + WAIT_ORDER(S)
    bh = [hops(xb, (s + S - j) % S, bx_s, bx_r, i) for i, j in enumerate(b_list)]
    ah = [hops(xa, c, ax_s, ax_r, c) for c in range(S)]

    xos = [
        remote(xb.at[0, (s + S - j) % S], xo.at[(s + S - j) % S], xo_s.at[i], xo_r.at[i], dp=1 - d)
        for i, j in enumerate(b_list)
    ]

    def b_piece(i):
        j = b_list[i]
        if j:
            src = (s + S - j) % S
            remote(arranged.at[j], xb.at[0, src], ex_s.at[j], ex_r.at[j], section=src).wait_recv()
        bh[i][1].start()
        bh[i][0].start()
        xos[i].start()

    def b_pass(i):
        bh[i][1].wait_recv()
        bh[i][2].start()

    def a_piece(c):
        if c == 0:
            @pl.when(s == 0)
            def _():
                emb_copy.wait()

        @pl.when(s > 0)
        def _():
            az[c].wait_recv()
        ah[c][1].start()
        ah[c][0].start()

    def a_pass(c):
        ah[c][1].wait_recv()
        ah[c][2].start()

    def forward(x, r, acc, first):
        lhs = x.at[r]

        def body(n, carry):
            at = pl.ds(pl.multiple_of(n * tile, tile), tile)
            val = dot_nn(lhs[...].reshape(rows, cols), w[r, :, at])
            if first:
                acc[n] = val
            else:
                acc[n] = acc[n] + val
            return carry
        lax.fori_loop(0, tiles, body, 0)

    def low_of(x, r):
        return dot_nn(x[r].reshape(rows, cols), dn[r])

    for i in range(S):
        b_piece(i)
        if i >= 1:
            b_pass(i - 1)

    d_copies[0].wait()
    w_copies[0].wait()
    forward(xb, 0, u, True)
    h = low_of(xb, 0)
    b_pass(S - 1)
    a_piece(0)
    for i in range(S):
        bh[i][0].wait_recv()
    d_copies[1].wait()
    w_copies[1].wait()
    forward(xb, 1, u, False)
    h = h + low_of(xb, 1)
    a_piece(1)
    d_copies[2].wait()
    w_copies[2].wait()
    forward(xb, 2, u, False)
    h = h + low_of(xb, 2)
    for i in range(S):
        bh[i][2].wait_recv()
    d_copies[3].wait()
    w_copies[3].wait()
    forward(xb, 3, u, False)
    h = h + low_of(xb, 3)
    hb[...] = h.astype(BF16)
    up_copy.wait()

    def slope_body(n, carry):
        at = pl.ds(pl.multiple_of(n * tile, tile), tile)
        unused, slope = gelu_pair(u[n] + dot_nn(hb[...], upv[:, at]))
        u[n] = slope
        return carry
    lax.fori_loop(0, tiles, slope_body, 0)
    a_pass(0)
    for c in range(2, S):
        a_piece(c)
        a_pass(c - 1)

    @pl.when(s == S - 1)
    def _():
        loss_copy.wait()

    @pl.when(s < S - 1)
    def _():
        gz.wait_recv()

    def scale_body(n, carry):
        at = pl.ds(pl.multiple_of(n * tile, tile), tile)
        scaled[:, at] = (g[:, :, at].reshape(rows, tile).astype(F32) * u[n]).astype(BF16)
        return carry
    lax.fori_loop(0, tiles, scale_body, 0)

    low[...] = dot_nt(scaled[...], upv[...]).astype(BF16)
    lows = [None] + [
        remote(low, lowr.at[r], low_s.at[r], low_r.at[r], tensor=rel[r]) for r in range(1, 4)
    ]
    for r in (2, 3, 1):
        lows[r].start()

    def partial(r, n):
        at = pl.ds(pl.multiple_of(n * tile, tile), tile)
        return dot_nt(scaled[...], w[r, at, :]) + dot_nt(low[...], dn[r, at, :])

    def p_copy(n):
        return remote(p_send.at[n], p_recv.at[n], p_s.at[n], p_r.at[n], tensor=t1)

    def q_copy(n):
        return remote(q_send.at[n], q_recv.at[n], q_s.at[n], q_r.at[n], tensor=t2)

    def o_copy(n):
        return remote(o_send.at[n], o_recv.at[n], o_s.at[n], o_r.at[n], tensor=t1)

    def p_body(n, carry):
        p_send[n] = partial(3, n).astype(BF16)
        p_copy(n).start()
        return carry
    lax.fori_loop(0, tiles, p_body, 0)

    def up_body(n, carry):
        at = pl.ds(pl.multiple_of(n * tile, tile), tile)
        du_send[:, at] = dot_tn(hb[...], scaled[:, at]).astype(BF16)
        return carry
    lax.fori_loop(0, tiles, up_body, 0)
    du = remote(du_send, du_recv, dp_s.at[0], dp_r.at[0], dp=1 - d)
    du.start()

    def q_body(n, carry):
        mine = partial(2, n)
        p_copy(n).wait_recv()
        q_send[n] = (mine + p_recv[n].astype(F32)).astype(BF16)
        q_copy(n).start()
        return carry
    lax.fori_loop(0, tiles, q_body, 0)
    a_pass(S - 1)

    total = low[...].astype(F32)
    for r in range(1, 4):
        lows[r].wait_recv()
        total = total + lowr[r].astype(F32)
    lg[...] = total.astype(BF16)
    dd = remote(lg, lg_recv, dp_s.at[1], dp_r.at[1], dp=1 - d)
    dd.start()

    def o_body(n, carry):
        o_send[n] = partial(1, n).astype(BF16)
        o_copy(n).start()
        return carry
    lax.fori_loop(0, tiles, o_body, 0)

    def own_body(n, carry):
        own[n] = partial(0, n)
        return carry
    lax.fori_loop(0, tiles, own_body, 0)

    forward(xa, 0, ua, True)
    h = low_of(xa, 0)
    for c in range(S):
        ah[c][0].wait_recv()
    forward(xa, 1, ua, False)
    h = h + low_of(xa, 1)
    forward(xa, 2, ua, False)
    h = h + low_of(xa, 2)
    for c in range(S):
        ah[c][2].wait_recv()
    forward(xa, 3, ua, False)
    h = h + low_of(xa, 3)
    ha = h.astype(BF16)
    hb2 = lowr.at[1]
    hb2[...] = ha

    def out_body(n, carry):
        at = pl.ds(pl.multiple_of(n * tile, tile), tile)
        value, unused = gelu_pair(ua[n] + dot_nn(lowr[1], upv[:, at]))
        base = xa[0, :, :, at].reshape(rows, tile).astype(F32)
        out_f[:, at] = (base + value).astype(BF16)
        return carry
    lax.fori_loop(0, tiles, out_body, 0)

    du.wait_recv()
    out_u[...] = (du_send[...].astype(F32) + du_recv[...].astype(F32)).astype(BF16)

    for i in range(S):
        xos[i].wait_recv()
    dd.wait_recv()
    here = dot_tn(xb[0].reshape(rows, cols), lg[...]).astype(BF16)
    there = dot_tn(xo[...].reshape(rows, cols), lg_recv[...]).astype(BF16)
    out_d[...] = (here.astype(F32) + there.astype(F32)).astype(BF16)

    for n in range(tiles):
        o_copy(n).wait_recv()
        q_copy(n).wait_recv()
        at = pl.ds(n * tile, tile)
        total = own[n] + o_recv[n].astype(F32) + q_recv[n].astype(F32)
        out_b[:, at] = (g[:, :, at].reshape(rows, tile).astype(F32) + total).astype(BF16)

    for j in range(1, S):
        ex[j].wait_send()

    @pl.when(s < S - 1)
    def _():
        for c in range(S):
            az[c].wait_send()

    @pl.when(s > 0)
    def _():
        gz.wait_send()
    for i in range(S):
        xos[i].wait_send()
        for hop in range(3):
            bh[i][hop].wait_send()
            ah[i][hop].wait_send()
    for r in range(1, 4):
        lows[r].wait_send()
    for n in range(tiles):
        p_copy(n).wait_send()
        q_copy(n).wait_send()
        o_copy(n).wait_send()
    du.wait_send()
    dd.wait_send()


def finish_kernel(*refs):
    sems, count = refs[-1], (len(refs) - 1) // 2
    copies = [
        pltpu.make_async_copy(refs[i], refs[count + i], sems.at[i]) for i in range(count)
    ]
    for copy in copies:
        copy.start()
    for copy in copies:
        copy.wait()


def EX_ORDER(S):
    return sorted(range(1, S), key=lambda j: (-min(j, S - j), j))


def WAIT_ORDER(S):
    return sorted(range(1, S), key=lambda j: (min(j, S - j), j))


def fused_on_device(sent, stash, table, embedded, loss, weight, down, up):
    S = lax.axis_size("section")
    piece, cols = stash.shape[1], stash.shape[2]
    rows, rank = S * piece, up.shape[1]
    tile = next(k for k in (512, 256, 128) if cols % k == 0)
    tiles = cols // tile
    any_space = pl.BlockSpec(memory_space=pl.ANY)
    hbm = pl.BlockSpec(memory_space=pltpu.HBM)
    vmem = pl.BlockSpec(memory_space=pltpu.VMEM)
    smem = pl.BlockSpec(memory_space=pltpu.SMEM)
    V = pltpu.VMEM
    dma = lambda *shape: pltpu.SemaphoreType.DMA(shape)
    block = (tiles, rows, tile)
    outs = pl.pallas_call(
        functools.partial(window_kernel, S, tile),
        out_shape=(
            jax.ShapeDtypeStruct((rows, cols), BF16),
            jax.ShapeDtypeStruct((rows, cols), BF16),
            jax.ShapeDtypeStruct((cols, rank), BF16),
            jax.ShapeDtypeStruct((rank, cols), BF16),
        ),
        in_specs=[hbm, hbm, smem, hbm, hbm, hbm, hbm, hbm],
        out_specs=(vmem,) * 4,
        scratch_shapes=[
            V((S, piece, cols), BF16), V((4, cols, cols), BF16), V((4, cols, rank), BF16), V((rank, cols), BF16),
            V((4, S, piece, cols), BF16), V((4, S, piece, cols), BF16),
            V((S, piece, cols), BF16), V((S, piece, cols), BF16),
            V(block, F32), V(block, F32), V((rows, cols), BF16),
            V((rows, rank), BF16), V((4, rows, rank), BF16), V((rows, rank), BF16),
            V(block, BF16), V(block, BF16), V(block, BF16),
            V(block, BF16), V(block, BF16), V(block, BF16), V(block, F32),
            V((rank, cols), BF16), V((rank, cols), BF16),
            V((S, piece, cols), BF16), V((rows, rank), BF16), V((rows, rank), BF16),
            dma(4), dma(4), dma(4), dma(S), dma(S), dma(S), dma(S), dma(1), dma(1), dma(S), dma(S),
            dma(3, S), dma(3, S), dma(3, S), dma(3, S), dma(4), dma(4),
            dma(tiles), dma(tiles), dma(tiles), dma(tiles), dma(tiles), dma(tiles),
            dma(2), dma(2),
        ],
        compiler_params=pltpu.CompilerParams(
            collective_id=0, has_side_effects=True, vmem_limit_bytes=60 * 1024 * 1024),
    )(
        sent.reshape(2, S, piece, cols), stash, table,
        embedded.reshape(S, piece, cols), loss.reshape(S, piece, cols),
        weight.reshape(4, cols, cols), down.reshape(4, cols, rank), up[0],
    )
    outs = pl.pallas_call(
        finish_kernel,
        out_shape=tuple(jax.ShapeDtypeStruct(o.shape, o.dtype) for o in outs),
        in_specs=(vmem,) * 4,
        out_specs=(any_space,) * 4,
        scratch_shapes=[dma(4)],
        compiler_params=pltpu.CompilerParams(vmem_limit_bytes=8 * 1024 * 1024),
    )(*outs)
    return tuple(o[None] for o in outs)


def solution(mesh):
    placed = (
        P("section", "dp", "tensor"),
        P("section", "dp", "tensor"),
        P("section", None),
        P("dp", "tensor"),
        P("dp", "tensor"),
        P("section", None, "tensor"),
        P("section", None, None),
        P("section", None, "tensor"),
    )
    def program(*args):
        rows = args[1].shape[1] // mesh.shape["dp"]
        cols = args[1].shape[2] // mesh.shape["tensor"]
        fits = (
            mesh.shape["tensor"] == 4 and mesh.shape["dp"] == 2
            and rows % 16 == 0 and cols % 128 == 0
        )
        return sharded(fused_on_device if fits else on_device)(*args)

    def sharded(body):
      return jax.shard_map(
        body,
        mesh=mesh,
        in_specs=placed,
        out_specs=(
            P("section", "dp", "tensor"),
            P("section", "dp", "tensor"),
            P("section", "tensor", None),
            P("section", None, "tensor"),
        ),
        check_vma=False,
    )

    return program
```

```python
import functools

import jax
import jax.numpy as jnp
from jax import lax
from jax.experimental import pallas as pl
from jax.experimental.pallas import tpu as pltpu
from jax.sharding import PartitionSpec as P

coef = 0.7978845608028654


def shifted(block, axis, distance):
    devices = range(lax.axis_size(axis))
    route = [(i - distance, i) for i in devices if i - distance in devices]
    return lax.ppermute(block, axis, route)


def gelu_pair(u):
    inner = coef * (u + 0.044715 * u * u * u)
    tanh_v = jnp.tanh(inner)
    value = 0.5 * u * (1.0 + tanh_v)
    slope = 0.5 * (1.0 + tanh_v) + 0.5 * u * (1.0 - tanh_v * tanh_v) * coef * (
        1.0 + 3.0 * 0.044715 * u * u
    )
    return (value, slope)


def on_device(
    sent,
    stashed_inputs,
    table,
    embedded,
    loss_gradient,
    weight,
    adapter_down_weight,
    adapter_up_weight,
):
    section = lax.axis_index("section")
    sections = lax.axis_size("section")
    w_section = weight[0]
    down_matrix = adapter_down_weight[0]
    up_matrix = adapter_up_weight[0]
    below = shifted(sent[1], "section", 1)
    above = shifted(sent[0], "section", -1)
    forward_input = jnp.where(section == 0, embedded, below)
    incoming_gradient = jnp.where(section == sections - 1, loss_gradient, above)
    order = jnp.argsort(table[0])
    arranged = jnp.take(stashed_inputs, order, axis=0)
    fetched = lax.all_to_all(arranged, "section", split_axis=0, concat_axis=0, tiled=True)
    backward_input = fetched.reshape(-1, fetched.shape[-1])
    full_a, full_b = (
        lax.all_gather(forward_input, "tensor", axis=1, tiled=True),
        lax.all_gather(backward_input, "tensor", axis=1, tiled=True),
    )
    main_a = jnp.dot(full_a, w_section, preferred_element_type=jnp.float32)
    h_a = jnp.dot(full_a, down_matrix, preferred_element_type=jnp.float32).astype(jnp.bfloat16)
    u_a = main_a + jnp.dot(h_a, up_matrix, preferred_element_type=jnp.float32)
    value_a, unused = gelu_pair(u_a)
    forward_output = (forward_input.astype(jnp.float32) + value_a).astype(jnp.bfloat16)
    h_b = jnp.dot(full_b, down_matrix, preferred_element_type=jnp.float32).astype(jnp.bfloat16)
    u_b = jnp.dot(full_b, w_section, preferred_element_type=jnp.float32) + jnp.dot(
        h_b, up_matrix, preferred_element_type=jnp.float32
    )
    unused_b, slope_b = gelu_pair(u_b)
    scaled = (incoming_gradient.astype(jnp.float32) * slope_b).astype(jnp.bfloat16)
    low_part = lax.dot_general(
        scaled, up_matrix, (((1,), (1,)), ((), ())), preferred_element_type=jnp.float32
    )
    low_piece = low_part.astype(jnp.bfloat16)
    partial_value = lax.dot_general(
        scaled, w_section, (((1,), (1,)), ((), ())), preferred_element_type=jnp.float32
    )
    partial_value = partial_value + lax.dot_general(
        low_piece, down_matrix, (((1,), (1,)), ((), ())), preferred_element_type=jnp.float32
    )
    input_grad = lax.psum_scatter(
        partial_value.astype(jnp.bfloat16), "tensor", scatter_dimension=1, tiled=True
    ).astype(jnp.float32)
    backward_output = (incoming_gradient.astype(jnp.float32) + input_grad).astype(jnp.bfloat16)
    low_grad = lax.psum(low_part.astype(jnp.bfloat16), "tensor")
    down_term = lax.dot_general(
        backward_input, low_grad, (((0,), (0,)), ((), ())), preferred_element_type=jnp.float32
    )
    up_term = lax.dot_general(
        h_b, scaled, (((0,), (0,)), ((), ())), preferred_element_type=jnp.float32
    )
    down_sum, up_sum = (
        lax.psum(down_term.astype(jnp.bfloat16), "dp").astype(jnp.float32),
        lax.psum(up_term.astype(jnp.bfloat16), "dp").astype(jnp.float32),
    )
    down_gradient = down_sum.astype(jnp.bfloat16)
    up_gradient = up_sum.astype(jnp.bfloat16)
    return (forward_output[None], backward_output[None], down_gradient[None], up_gradient[None])


F32 = jnp.float32
BF16 = jnp.bfloat16
MESH = pl.DeviceIdType.MESH


def dot_nn(a, b):
    return lax.dot_general(a, b, (((1,), (0,)), ((), ())), preferred_element_type=F32)


def dot_nt(a, b):
    return lax.dot_general(a, b, (((1,), (1,)), ((), ())), preferred_element_type=F32)


def dot_tn(a, b):
    return lax.dot_general(a, b, (((0,), (0,)), ((), ())), preferred_element_type=F32)


def window_kernel(
    sections, tile,
    sent, stash_hbm, table, embedded, loss, weight, down, up,
    out_f, out_b, out_d, out_u,
    stash_v, w, dn, upv, xa, xb, g, arranged, u, ua, scaled, low, lowr, hb,
    p_send, q_send, o_send, p_recv, q_recv, o_recv, own,
    du_send, du_recv, xo, lg, lg_recv,
    w_sem, d_sem, loc_sem, ex_s, ex_r, az_s, az_r, gz_s, gz_r,
    xo_s, xo_r, bx_s, bx_r, ax_s, ax_r, low_s, low_r, p_s, p_r, q_s, q_r, o_s, o_r, dp_s, dp_r,
):
    S = sections
    s = lax.axis_index("section")
    d = lax.axis_index("dp")
    t = lax.axis_index("tensor")
    t1 = t + 1 - 2 * (t % 2)
    t2 = (t + 2) % 4
    t3 = (t1 + 2) % 4
    rel = [t, t1, t2, t3]
    piece, cols = stash_v.shape[1], stash_v.shape[2]
    rows = S * piece
    tiles = cols // tile
    stash_copy = pltpu.make_async_copy(stash_hbm, stash_v, loc_sem.at[0])
    stash_copy.start()

    def remote(src, dst, ss, rs, **device):
        return pltpu.make_async_remote_copy(
            src_ref=src, dst_ref=dst, send_sem=ss, recv_sem=rs,
            device_id=device, device_id_type=MESH)

    emb_copy = pltpu.make_async_copy(embedded, xa.at[0], loc_sem.at[3])
    loss_copy = pltpu.make_async_copy(loss, g, loc_sem.at[1])
    up_copy = pltpu.make_async_copy(up, upv, loc_sem.at[2])
    w_copies = [pltpu.make_async_copy(weight.at[rel[r]], w.at[r], w_sem.at[r]) for r in range(4)]
    d_copies = [pltpu.make_async_copy(down.at[rel[r]], dn.at[r], d_sem.at[r]) for r in range(4)]

    barrier = pltpu.get_barrier_semaphore()
    for j in range(1, S):
        pl.semaphore_signal(barrier, inc=1, device_id={"section": (s + j) % S}, device_id_type=MESH)
    for r in range(1, 4):
        pl.semaphore_signal(barrier, inc=1, device_id={"tensor": rel[r]}, device_id_type=MESH)
    pl.semaphore_signal(barrier, inc=1, device_id={"dp": 1 - d}, device_id_type=MESH)

    stash_copy.wait()
    for j in range(S):
        dest = (s + j) % S
        k = jnp.int32(0)
        for i in range(S):
            k = jnp.where(table[0, i] == dest, i, k)
        if j == 0:
            xb[0, s] = stash_v[k]
        else:
            arranged[j] = stash_v[k]
    pl.semaphore_wait(barrier, S + 3)

    ex = [None] + [
        remote(arranged.at[j], xb.at[0, s], ex_s.at[j], ex_r.at[j], section=(s + j) % S)
        for j in range(1, S)
    ]
    for j in EX_ORDER(S):
        ex[j].start()

    @pl.when(s == 0)
    def _():
        emb_copy.start()

    @pl.when(s == S - 1)
    def _():
        loss_copy.start()

    for r in range(4):
        d_copies[r].start()
        w_copies[r].start()
    up_copy.start()

    az = [remote(sent.at[1, c], xa.at[0, c], az_s.at[c], az_r.at[c], section=(s + 1) % S) for c in range(S)]
    gz = remote(sent.at[0], g, gz_s.at[0], gz_r.at[0], section=(s + S - 1) % S)

    @pl.when(s < S - 1)
    def _():
        for c in range(S):
            az[c].start()

    @pl.when(s > 0)
    def _():
        gz.start()

    def hops(x, c, sem_s, sem_r, i):
        return (
            remote(x.at[0, c], x.at[1, c], sem_s.at[0, i], sem_r.at[0, i], tensor=t1),
            remote(x.at[0, c], x.at[2, c], sem_s.at[1, i], sem_r.at[1, i], tensor=t2),
            remote(x.at[2, c], x.at[3, c], sem_s.at[2, i], sem_r.at[2, i], tensor=t1),
        )

    b_list = [0] + WAIT_ORDER(S)
    bh = [hops(xb, (s + S - j) % S, bx_s, bx_r, i) for i, j in enumerate(b_list)]
    ah = [hops(xa, c, ax_s, ax_r, c) for c in range(S)]

    xos = [
        remote(xb.at[0, (s + S - j) % S], xo.at[(s + S - j) % S], xo_s.at[i], xo_r.at[i], dp=1 - d)
        for i, j in enumerate(b_list)
    ]

    def b_piece(i):
        j = b_list[i]
        if j:
            src = (s + S - j) % S
            remote(arranged.at[j], xb.at[0, src], ex_s.at[j], ex_r.at[j], section=src).wait_recv()
        bh[i][1].start()
        bh[i][0].start()
        xos[i].start()

    def b_pass(i):
        bh[i][1].wait_recv()
        bh[i][2].start()

    def a_piece(c):
        if c == 0:
            @pl.when(s == 0)
            def _():
                emb_copy.wait()

        @pl.when(s > 0)
        def _():
            az[c].wait_recv()
        ah[c][1].start()
        ah[c][0].start()

    def a_pass(c):
        ah[c][1].wait_recv()
        ah[c][2].start()

    def forward(x, r, acc, first):
        lhs = x.at[r]

        def body(n, carry):
            at = pl.ds(pl.multiple_of(n * tile, tile), tile)
            val = dot_nn(lhs[...].reshape(rows, cols), w[r, :, at])
            if first:
                acc[n] = val
            else:
                acc[n] = acc[n] + val
            return carry
        lax.fori_loop(0, tiles, body, 0)

    def low_of(x, r):
        return dot_nn(x[r].reshape(rows, cols), dn[r])

    for i in range(S):
        b_piece(i)
        if i >= 1:
            b_pass(i - 1)

    d_copies[0].wait()
    w_copies[0].wait()
    forward(xb, 0, u, True)
    h = low_of(xb, 0)
    b_pass(S - 1)
    a_piece(0)
    for i in range(S):
        bh[i][0].wait_recv()
    d_copies[1].wait()
    w_copies[1].wait()
    forward(xb, 1, u, False)
    h = h + low_of(xb, 1)
    a_piece(1)
    d_copies[2].wait()
    w_copies[2].wait()
    forward(xb, 2, u, False)
    h = h + low_of(xb, 2)
    for i in range(S):
        bh[i][2].wait_recv()
    d_copies[3].wait()
    w_copies[3].wait()
    forward(xb, 3, u, False)
    h = h + low_of(xb, 3)
    hb[...] = h.astype(BF16)
    up_copy.wait()

    def slope_body(n, carry):
        at = pl.ds(pl.multiple_of(n * tile, tile), tile)
        unused, slope = gelu_pair(u[n] + dot_nn(hb[...], upv[:, at]))
        u[n] = slope
        return carry
    lax.fori_loop(0, tiles, slope_body, 0)
    a_pass(0)
    for c in range(2, S):
        a_piece(c)
        a_pass(c - 1)

    @pl.when(s == S - 1)
    def _():
        loss_copy.wait()

    @pl.when(s < S - 1)
    def _():
        gz.wait_recv()

    def scale_body(n, carry):
        at = pl.ds(pl.multiple_of(n * tile, tile), tile)
        scaled[:, at] = (g[:, :, at].reshape(rows, tile).astype(F32) * u[n]).astype(BF16)
        return carry
    lax.fori_loop(0, tiles, scale_body, 0)

    low[...] = dot_nt(scaled[...], upv[...]).astype(BF16)
    lows = [None] + [
        remote(low, lowr.at[r], low_s.at[r], low_r.at[r], tensor=rel[r]) for r in range(1, 4)
    ]
    for r in (2, 3, 1):
        lows[r].start()

    def partial(r, n):
        at = pl.ds(pl.multiple_of(n * tile, tile), tile)
        return dot_nt(scaled[...], w[r, at, :]) + dot_nt(low[...], dn[r, at, :])

    def p_copy(n):
        return remote(p_send.at[n], p_recv.at[n], p_s.at[n], p_r.at[n], tensor=t1)

    def q_copy(n):
        return remote(q_send.at[n], q_recv.at[n], q_s.at[n], q_r.at[n], tensor=t2)

    def o_copy(n):
        return remote(o_send.at[n], o_recv.at[n], o_s.at[n], o_r.at[n], tensor=t1)

    def p_body(n, carry):
        p_send[n] = partial(3, n).astype(BF16)
        p_copy(n).start()
        return carry
    lax.fori_loop(0, tiles, p_body, 0)

    def up_body(n, carry):
        at = pl.ds(pl.multiple_of(n * tile, tile), tile)
        du_send[:, at] = dot_tn(hb[...], scaled[:, at]).astype(BF16)
        return carry
    lax.fori_loop(0, tiles, up_body, 0)
    du = remote(du_send, du_recv, dp_s.at[0], dp_r.at[0], dp=1 - d)
    du.start()

    def q_body(n, carry):
        mine = partial(2, n)
        p_copy(n).wait_recv()
        q_send[n] = (mine + p_recv[n].astype(F32)).astype(BF16)
        q_copy(n).start()
        return carry
    lax.fori_loop(0, tiles, q_body, 0)
    a_pass(S - 1)

    total = low[...].astype(F32)
    for r in range(1, 4):
        lows[r].wait_recv()
        total = total + lowr[r].astype(F32)
    lg[...] = total.astype(BF16)
    dd = remote(lg, lg_recv, dp_s.at[1], dp_r.at[1], dp=1 - d)
    dd.start()

    def o_body(n, carry):
        o_send[n] = partial(1, n).astype(BF16)
        o_copy(n).start()
        return carry
    lax.fori_loop(0, tiles, o_body, 0)

    def own_body(n, carry):
        own[n] = partial(0, n)
        return carry
    lax.fori_loop(0, tiles, own_body, 0)

    forward(xa, 0, ua, True)
    h = low_of(xa, 0)
    for c in range(S):
        ah[c][0].wait_recv()
    forward(xa, 1, ua, False)
    h = h + low_of(xa, 1)
    forward(xa, 2, ua, False)
    h = h + low_of(xa, 2)
    for c in range(S):
        ah[c][2].wait_recv()
    forward(xa, 3, ua, False)
    h = h + low_of(xa, 3)
    ha = h.astype(BF16)
    hb2 = lowr.at[1]
    hb2[...] = ha

    def out_body(n, carry):
        at = pl.ds(pl.multiple_of(n * tile, tile), tile)
        value, unused = gelu_pair(ua[n] + dot_nn(lowr[1], upv[:, at]))
        base = xa[0, :, :, at].reshape(rows, tile).astype(F32)
        out_f[:, at] = (base + value).astype(BF16)
        return carry
    lax.fori_loop(0, tiles, out_body, 0)

    du.wait_recv()
    out_u[...] = (du_send[...].astype(F32) + du_recv[...].astype(F32)).astype(BF16)

    for i in range(S):
        xos[i].wait_recv()
    dd.wait_recv()
    here = dot_tn(xb[0].reshape(rows, cols), lg[...]).astype(BF16)
    there = dot_tn(xo[...].reshape(rows, cols), lg_recv[...]).astype(BF16)
    out_d[...] = (here.astype(F32) + there.astype(F32)).astype(BF16)

    for n in range(tiles):
        o_copy(n).wait_recv()
        q_copy(n).wait_recv()
        at = pl.ds(n * tile, tile)
        total = own[n] + o_recv[n].astype(F32) + q_recv[n].astype(F32)
        out_b[:, at] = (g[:, :, at].reshape(rows, tile).astype(F32) + total).astype(BF16)

    for j in range(1, S):
        ex[j].wait_send()

    @pl.when(s < S - 1)
    def _():
        for c in range(S):
            az[c].wait_send()

    @pl.when(s > 0)
    def _():
        gz.wait_send()
    for i in range(S):
        xos[i].wait_send()
        for hop in range(3):
            bh[i][hop].wait_send()
            ah[i][hop].wait_send()
    for r in range(1, 4):
        lows[r].wait_send()
    for n in range(tiles):
        p_copy(n).wait_send()
        q_copy(n).wait_send()
        o_copy(n).wait_send()
    du.wait_send()
    dd.wait_send()


def EX_ORDER(S):
    return sorted(range(1, S), key=lambda j: (-min(j, S - j), j))


def WAIT_ORDER(S):
    return sorted(range(1, S), key=lambda j: (min(j, S - j), j))


def fused_on_device(sent, stash, table, embedded, loss, weight, down, up):
    S = lax.axis_size("section")
    piece, cols = stash.shape[1], stash.shape[2]
    rows, rank = S * piece, up.shape[1]
    tile = next(k for k in (768, 512, 256, 128) if cols % k == 0)
    tiles = cols // tile
    any_space = pl.BlockSpec(memory_space=pl.ANY)
    hbm = pl.BlockSpec(memory_space=pltpu.HBM)
    vmem = pl.BlockSpec(memory_space=pltpu.VMEM)
    smem = pl.BlockSpec(memory_space=pltpu.SMEM)
    V = pltpu.VMEM
    dma = lambda *shape: pltpu.SemaphoreType.DMA(shape)
    block = (tiles, rows, tile)
    outs = pl.pallas_call(
        functools.partial(window_kernel, S, tile),
        out_shape=(
            jax.ShapeDtypeStruct((rows, cols), BF16),
            jax.ShapeDtypeStruct((rows, cols), BF16),
            jax.ShapeDtypeStruct((cols, rank), BF16),
            jax.ShapeDtypeStruct((rank, cols), BF16),
        ),
        in_specs=[hbm, hbm, smem, hbm, hbm, hbm, hbm, hbm],
        out_specs=(vmem,) * 4,
        scratch_shapes=[
            V((S, piece, cols), BF16), V((4, cols, cols), BF16), V((4, cols, rank), BF16), V((rank, cols), BF16),
            V((4, S, piece, cols), BF16), V((4, S, piece, cols), BF16),
            V((S, piece, cols), BF16), V((S, piece, cols), BF16),
            V(block, F32), V(block, F32), V((rows, cols), BF16),
            V((rows, rank), BF16), V((4, rows, rank), BF16), V((rows, rank), BF16),
            V(block, BF16), V(block, BF16), V(block, BF16),
            V(block, BF16), V(block, BF16), V(block, BF16), V(block, F32),
            V((rank, cols), BF16), V((rank, cols), BF16),
            V((S, piece, cols), BF16), V((rows, rank), BF16), V((rows, rank), BF16),
            dma(4), dma(4), dma(4), dma(S), dma(S), dma(S), dma(S), dma(1), dma(1), dma(S), dma(S),
            dma(3, S), dma(3, S), dma(3, S), dma(3, S), dma(4), dma(4),
            dma(tiles), dma(tiles), dma(tiles), dma(tiles), dma(tiles), dma(tiles),
            dma(2), dma(2),
        ],
        compiler_params=pltpu.CompilerParams(
            collective_id=0, has_side_effects=True, vmem_limit_bytes=60 * 1024 * 1024),
    )(
        sent.reshape(2, S, piece, cols), stash, table,
        embedded.reshape(S, piece, cols), loss.reshape(S, piece, cols),
        weight.reshape(4, cols, cols), down.reshape(4, cols, rank), up[0],
    )
    return tuple(o[None] for o in outs)


def solution(mesh):
    placed = (
        P("section", "dp", "tensor"),
        P("section", "dp", "tensor"),
        P("section", None),
        P("dp", "tensor"),
        P("dp", "tensor"),
        P("section", None, "tensor"),
        P("section", None, None),
        P("section", None, "tensor"),
    )
    def program(*args):
        rows = args[1].shape[1] // mesh.shape["dp"]
        cols = args[1].shape[2] // mesh.shape["tensor"]
        fits = (
            mesh.shape["tensor"] == 4 and mesh.shape["dp"] == 2
            and rows % 16 == 0 and cols % 128 == 0
        )
        return sharded(fused_on_device if fits else on_device)(*args)

    def sharded(body):
      return jax.shard_map(
        body,
        mesh=mesh,
        in_specs=placed,
        out_specs=(
            P("section", "dp", "tensor"),
            P("section", "dp", "tensor"),
            P("section", "tensor", None),
            P("section", None, "tensor"),
        ),
        check_vma=False,
    )

    return program
```
